32 devices in a mesh: expert: 4 (over y, core), dp: 8 (over z, x).
Axes of the slice: x: 2, y: 2, z: 4, core: 2. Of those that a mesh axis runs over, the one named last changes fastest.
Arguments:
- tokens: bfloat16 [2048, 3584], P(('dp', 'expert')), parts along dimension 0, may hold values from -6 to 6
- expert_ids: int32 [2048, 1], P(('dp', 'expert')), parts along dimension 0, may hold values from 0 to 3; in each aligned block of 64 rows (0 to 63, 64 to 127, ...) at most 18 rows name the same one
- combine: bfloat16 [2048, 1], P(('dp', 'expert')), parts along dimension 0, may hold values from 0.19921875 to 1
- w_gate: bfloat16 [3584, 8192], P(None, 'expert'), may hold values from -0.09375 to 0.09375
- w_up: bfloat16 [3584, 8192], P(None, 'expert'), may hold values from -0.09375 to 0.09375
- w_down: bfloat16 [8192, 3584], P('expert'), may hold values from -0.125 to 0.125
Outputs:
- mixed: bfloat16 [2048, 3584], P(('dp', 'expert')), parts along dimension 0
The draws below stay inside these ranges and needn't reach their ends.
There are 8 independent parts, one for each index of `dp`. The reference program is written for one: setup_inputs(seed, part) draws one part's arguments, and reference() takes and returns one part's arrays. A program takes and returns all parts, laid end to end along the dimension named above; an argument that names none is the same for every part. Nothing has to cross between parts.
Inputs may be any that keep to these rules, and one draw needn't show every extreme that they name: `expert_ids`: each token names one expert. Among the 64 tokens of one device (aligned blocks of rows) no expert is named more than 18 times, a bound that some block reaches.
All inputs are finite; a program needn't handle non-finite values.
Results may differ from the reference program's by a relative error of at most 0.0057.
Values may be sent and summed in bfloat16 or wider, within the bound.
A program may use at most 128 MiB of HBM per device.

```python
import math
import jax
import jax.numpy as jnp
import numpy as np
from jax import lax

D = 3584
HW = 2048
EXPERTS = 4
TOP = 1
TOK_DEV = 64
CAP = 18
TOKENS = 256
SLICE = 2048
N_EXPERT = 4


def block_scale(stream_key, dims, cuts, smallest, top_value):
    loudness, own = 1.0, jax.random.fold_in(stream_key, 6)
    for axis_at, blocks in cuts:
        draws = jnp.exp(jax.random.uniform(jax.random.fold_in(own, axis_at), (blocks,), jnp.float32, smallest / len(cuts), top_value / len(cuts)))
        loudness = loudness * jnp.repeat(draws, dims[axis_at] // blocks).reshape([-1 if axis == axis_at else 1 for axis in range(len(dims))])
    return loudness


def routed_block(own_key, own, number, rows, number_of, top, most, skew):
    order = jax.random.permutation(own_key, number_of)
    heavy_load, common = shares(number_of, rows * top, most, skew, True), shares(number_of, rows * top, most, skew, False)
    places = jnp.arange(number_of)

    def named(tallies, offset_by):
        used = int((tallies > 0).sum())
        fixed = max(1, used // 4)
        shifted = fixed + (places - fixed + offset_by * (used - fixed)) % max(1, number_of - fixed)
        return jnp.zeros((number_of,), jnp.int32).at[order[jnp.where(places < fixed, places, shifted)]].set(jnp.asarray(tallies, jnp.int32))

    tallies = jnp.where(number % 4 == 0, named(heavy_load, number // 4), named(common, number - number // 4 - 1))
    mixed = jax.random.permutation(jax.random.fold_in(own, 3), number_of)
    source_of, sink = mixed[0:number_of // 2 * 2:2], mixed[1:number_of // 2 * 2:2]
    margin = jnp.minimum(tallies[source_of] - 1, most - tallies[sink]) // 2
    margin = jnp.where((source_of == order[0]) | (sink == order[0]) | (tallies[sink] == 0), 0, jnp.maximum(margin, 0))
    shifted = jax.random.randint(jax.random.fold_in(own, 4), (number_of // 2,), 0, 1 << 20) % (margin + 1)
    tallies = tallies.at[source_of].add(-shifted).at[sink].add(shifted)
    labels = jnp.searchsorted(jnp.cumsum(tallies), jnp.arange(rows * top), side="right").astype(jnp.int32)
    grid = labels.reshape(top, rows).T
    grid = grid[jax.random.permutation(jax.random.fold_in(own, 1), rows)]
    offset_by = jax.random.randint(jax.random.fold_in(own, 2), (rows, 1), 0, top)
    return jnp.take_along_axis(grid, (jnp.arange(top)[None, :] + offset_by) % top, axis=1)


def shares(amount, total, reach, skew, full):
    portions = [(1 << 20) // math.isqrt(rank ** skew) + 1 for rank in range(1, amount + 1)]
    largest = reach if full else min(reach, max(-(-total // amount), total * portions[0] // sum(portions)))
    least = 1 if total - largest >= amount - 1 else 0
    holding, surplus = [largest] + [least] * (amount - 1), total - largest - least * (amount - 1)
    while surplus > 0:
        free = [i for i in range(1, amount) if holding[i] < largest] or [i for i in range(1, amount) if holding[i] < reach]
        mass, remaining = sum([portions[i] for i in free]), surplus
        for i in free:
            addition = min(reach - holding[i], max(1, remaining * portions[i] // mass), surplus)
            holding[i] = holding[i] + addition
            surplus = surplus - addition
    return np.array(holding)


def scatter_about(own_key, shape, scale, reach, split=(), held_as=jnp.bfloat16):
    entries = jax.random.normal(own_key, shape, jnp.float32) * scale
    if len(split) > 0:
        entries = block_scale(own_key, shape, split, -0.22, 0.18) * entries
    return jnp.clip(entries, min=-reach, max=reach).astype(held_as)


def setup_inputs(seed: int = 0, part: int = 0) -> dict:
    streams_of = jax.random.split(jax.random.key(seed), 7)
    part_keys = jax.random.split(jax.random.fold_in(streams_of[6], part), 7)
    tokens = scatter_about(part_keys[0], (TOKENS, D), 1.0, 6.0, ((0, 4),))
    expert_ids_keys = jax.random.split(jax.random.fold_in(part_keys[1], 1), TOKENS // TOK_DEV)
    expert_ids_turns = jax.random.permutation(jax.random.fold_in(part_keys[1], 3), TOKENS // TOK_DEV)
    expert_ids = jax.vmap(lambda own, number: routed_block(jax.random.fold_in(part_keys[1], 2), own, number, TOK_DEV, EXPERTS, TOP, CAP, 2))(expert_ids_keys, expert_ids_turns).reshape((TOKENS, TOP))
    combine = jnp.clip(0.19921875 + 0.80078125 * jax.random.uniform(part_keys[2], (TOKENS, TOP), jnp.float32) ** block_scale(part_keys[2], (TOKENS, TOP), ((0, 4),), -0.2, 0.2), 0.19921875, 1.0).astype(jnp.bfloat16)
    w_gate = scatter_about(streams_of[3], (D, EXPERTS * HW), D ** -0.5, 0.09375, ((1, 4),))
    w_up = scatter_about(streams_of[4], (D, EXPERTS * HW), D ** -0.5, 0.09375, ((1, 4),))
    w_down = scatter_about(streams_of[5], (EXPERTS * HW, D), HW ** -0.5, 0.125, ((0, 4),))
    return {"tokens": tokens, "expert_ids": expert_ids, "combine": combine, "w_gate": w_gate, "w_up": w_up, "w_down": w_down}


def reference(tokens, expert_ids, combine, w_gate, w_up, w_down):
    accumulated = jnp.zeros((TOKENS, D), jnp.float32)
    weight_table = combine.astype(jnp.float32)
    span_size = N_EXPERT // EXPERTS
    for e in range(EXPERTS):
        gate_values = jnp.dot(tokens, w_gate[:, e * HW:(e + 1) * HW], preferred_element_type=jnp.float32)
        up_values = jnp.dot(tokens, w_up[:, e * HW:(e + 1) * HW], preferred_element_type=jnp.float32)
        hidden = (jax.nn.silu(gate_values) * up_values).astype(jnp.bfloat16)
        slice_total = jnp.zeros((TOKENS, D), jnp.float32)
        for s in range(span_size):
            first_row = e * HW + s * SLICE
            piece_out = jnp.dot(hidden[:, s * SLICE:(s + 1) * SLICE], w_down[first_row:first_row + SLICE, :], preferred_element_type=jnp.float32).astype(jnp.bfloat16)
            slice_total = slice_total + lax.optimization_barrier(piece_out).astype(jnp.float32)
        row_weight = jnp.sum(weight_table * (expert_ids == e).astype(jnp.float32), axis=1)
        accumulated = accumulated + row_weight[:, None] * slice_total
    return accumulated.astype(jnp.bfloat16)
```

```python
import functools

import jax
import jax.numpy as jnp
from jax import lax
from jax.experimental import pallas as pl
from jax.experimental.pallas import tpu as pltpu
from jax.sharding import PartitionSpec as P

EXPERTS = 4
TOP = 1
CAP = 18
MAIN = 16
EXTRA = CAP - MAIN
FOLD = 8
LANES = 128
PIECES = FOLD // EXTRA
CHUNK = PIECES * LANES
BF16, F32, I32 = jnp.bfloat16, jnp.float32, jnp.int32


def iota(shape, axis):
    return lax.broadcasted_iota(I32, shape, axis)


def dot(a, b):
    return jnp.dot(a, b, preferred_element_type=F32)


def kernel(
    n, span, chunks, tokens_hbm, ids_hbm, combine_hbm, gate_hbm, up_hbm, down_hbm, out_hbm,
    tokens, ids, combine, gate, up, down, send_m, send_e, recv_m, recv_e, gate_sum, up_sum,
    hidden, out, back_m, back_e, home_m, home_e,
    small_sem, gate_sem, up_sem, down_sem, out_sem, send_sem, recv_sem, back_sem, home_sem,
):
    me = lax.axis_index("expert")
    count = tokens.shape[0]
    width = gate.shape[2]
    extra_rows = -(-EXTRA * n // MAIN) * MAIN
    chip, core = me // 2, me % 2

    peers = []
    for step in range(1, n // 2):
        for turn in range(2):
            peers.append((chip + step) % (n // 2) * 2 + (core + turn) % 2)
    peers.append(chip * 2 + (core + 1) % 2)

    barrier = pltpu.get_barrier_semaphore()
    for peer in peers:
        pl.semaphore_signal(barrier, inc=1, device_id={"expert": peer})

    first = [
        pltpu.make_async_copy(ids_hbm, ids, small_sem.at[0]),
        pltpu.make_async_copy(tokens_hbm, tokens, small_sem.at[1]),
        pltpu.make_async_copy(combine_hbm, combine, small_sem.at[2]),
    ]
    for copy in first:
        copy.start()

    def gate_copy(k):
        rows = pl.ds(pl.multiple_of(k * CHUNK, CHUNK), CHUNK)
        return pltpu.make_async_copy(gate_hbm.at[rows, :], gate.at[k], gate_sem.at[k])

    def up_copy(k):
        rows = pl.ds(pl.multiple_of(k * CHUNK, CHUNK), CHUNK)
        return pltpu.make_async_copy(up_hbm.at[rows, :], up.at[k], up_sem.at[k])

    def down_copy(k):
        columns = pl.ds(pl.multiple_of(k * CHUNK, CHUNK), CHUNK)
        return pltpu.make_async_copy(down_hbm.at[:, columns], down.at[k], down_sem.at[k])

    def out_copy(k):
        columns = pl.ds(pl.multiple_of(k * CHUNK, CHUNK), CHUNK)
        return pltpu.make_async_copy(out.at[k], out_hbm.at[:, columns], out_sem.at[k])

    def start_in(k, _):
        gate_copy(k).start()
        up_copy(k).start()
        return 0

    def start_down(k, _):
        down_copy(k).start()
        return 0

    lax.fori_loop(0, chunks, start_in, 0)
    lax.fori_loop(0, chunks, start_down, 0)

    first[0].wait()
    own = ids[...]
    member = iota((8, count), 0) == own
    earlier = (iota((count, count), 0) < iota((count, count), 1)).astype(F32).astype(BF16)
    ranks = dot(member.astype(F32).astype(BF16), earlier)
    place = jnp.sum(jnp.where(member, ranks, 0.0), axis=0, keepdims=True).astype(I32)
    low, high = own * span, own * span + span

    def main_mask():
        row = iota((n * MAIN, count), 0)
        block = row // MAIN
        return (block >= low) & (block < high) & (row - block * MAIN == place)

    def extra_mask(piece):
        row = iota((n * FOLD, count), 0)
        block = row // FOLD
        inner = row - block * FOLD - piece * EXTRA
        return (block >= low) & (block < high) & (inner >= 0) & (inner < EXTRA) & (inner + MAIN == place)

    pick_main = jnp.where(main_mask(), 1.0, 0.0).astype(BF16)
    pick_extra = [jnp.where(extra_mask(j), 1.0, 0.0).astype(BF16) for j in range(PIECES)]

    def send_copies(k, peer):
        return (
            pltpu.make_async_remote_copy(
                src_ref=send_m.at[k, peer], dst_ref=recv_m.at[k, me],
                send_sem=send_sem.at[k, peer, 0], recv_sem=recv_sem.at[k, me, 0],
                device_id={"expert": peer},
            ),
            pltpu.make_async_remote_copy(
                src_ref=send_e.at[k, peer], dst_ref=recv_e.at[k, me],
                send_sem=send_sem.at[k, peer, 1], recv_sem=recv_sem.at[k, me, 1],
                device_id={"expert": peer},
            ),
        )

    def arrivals(k, peer):
        return (
            pltpu.make_async_remote_copy(
                src_ref=send_m.at[k, peer], dst_ref=recv_m.at[k, peer],
                send_sem=send_sem.at[k, peer, 0], recv_sem=recv_sem.at[k, peer, 0],
                device_id={"expert": peer},
            ),
            pltpu.make_async_remote_copy(
                src_ref=send_e.at[k, peer], dst_ref=recv_e.at[k, peer],
                send_sem=send_sem.at[k, peer, 1], recv_sem=recv_sem.at[k, peer, 1],
                device_id={"expert": peer},
            ),
        )

    def back_copies(k, peer):
        return (
            pltpu.make_async_remote_copy(
                src_ref=back_m.at[k, peer], dst_ref=home_m.at[k, me],
                send_sem=back_sem.at[k, peer, 0], recv_sem=home_sem.at[k, me, 0],
                device_id={"expert": peer},
            ),
            pltpu.make_async_remote_copy(
                src_ref=back_e.at[k, peer], dst_ref=home_e.at[k, me],
                send_sem=back_sem.at[k, peer, 1], recv_sem=home_sem.at[k, me, 1],
                device_id={"expert": peer},
            ),
        )

    def returns(k, peer):
        return (
            pltpu.make_async_remote_copy(
                src_ref=back_m.at[k, peer], dst_ref=home_m.at[k, peer],
                send_sem=back_sem.at[k, peer, 0], recv_sem=home_sem.at[k, peer, 0],
                device_id={"expert": peer},
            ),
            pltpu.make_async_remote_copy(
                src_ref=back_e.at[k, peer], dst_ref=home_e.at[k, peer],
                send_sem=back_sem.at[k, peer, 1], recv_sem=home_sem.at[k, peer, 1],
                device_id={"expert": peer},
            ),
        )

    first[1].wait()
    pl.semaphore_wait(barrier, n - 1)

    def dispatch(k, _):
        base = pl.multiple_of(k * CHUNK, CHUNK)
        block = tokens[:, pl.ds(base, CHUNK)]
        send_m[k] = dot(pick_main, block).astype(BF16).reshape(n, MAIN, CHUNK)
        folded = sum(
            dot(pick_extra[j], block[:, j * LANES:(j + 1) * LANES]) for j in range(PIECES)
        )
        send_e[k] = folded.reshape(n, FOLD, LANES).astype(BF16)
        for peer in peers:
            for copy in send_copies(k, peer):
                copy.start()
        recv_m[k, me] = send_m[k, me]
        recv_e[k, me] = send_e[k, me]
        return 0

    lax.fori_loop(0, chunks, dispatch, 0)

    first[2].wait()
    weight = combine[...].astype(F32)
    put_main = jnp.transpose(jnp.where(main_mask(), weight, 0.0)).astype(BF16)
    put_extra = [
        jnp.transpose(jnp.where(extra_mask(j), weight, 0.0)).astype(BF16) for j in range(PIECES)
    ]

    def spread(j):
        row, column = iota((extra_rows, n * FOLD), 0), iota((extra_rows, n * FOLD), 1)
        source = row // EXTRA
        wanted = source * FOLD + j * EXTRA + (row - source * EXTRA)
        return jnp.where(column == wanted, 1.0, 0.0).astype(BF16)

    def fold(j):
        row, column = iota((n * FOLD, extra_rows), 0), iota((n * FOLD, extra_rows), 1)
        source = column // EXTRA
        wanted = source * FOLD + j * EXTRA + (column - source * EXTRA)
        return jnp.where(row == wanted, 1.0, 0.0).astype(BF16)

    spreads = [spread(j) for j in range(PIECES)]
    folds = [fold(j) for j in range(PIECES)]

    def gathered(k):
        for peer in peers:
            for copy in arrivals(k, peer):
                copy.wait_recv()
        extras = recv_e[k].astype(F32).reshape(n * FOLD, LANES).astype(BF16)
        tail = jnp.concatenate([dot(s, extras) for s in spreads], axis=1).astype(BF16)
        return jnp.concatenate([recv_m[k].reshape(n * MAIN, CHUNK), tail], axis=0)

    gate_sum[...] = jnp.zeros_like(gate_sum)
    up_sum[...] = jnp.zeros_like(up_sum)

    def project(k, _):
        rows = gathered(k)
        gate_copy(k).wait()
        gate_sum[...] += dot(rows, gate[k])
        up_copy(k).wait()
        up_sum[...] += dot(rows, up[k])
        return 0

    lax.fori_loop(0, chunks - 1, project, 0)
    last = chunks - 1
    rows = gathered(last)
    gate_copy(last).wait()
    up_copy(last).wait()
    tile = min(512, width)
    for at in range(0, width, tile):
        part = slice(at, at + tile)
        g = gate_sum[:, part] + dot(rows, gate[last, :, part])
        u = up_sum[:, part] + dot(rows, up[last, :, part])
        hidden[:, part] = (g / (1.0 + jnp.exp(-g)) * u).astype(BF16)

    def finish(k, _):
        down_copy(k).wait()
        result = dot(hidden[...], down[k])
        back_m[k] = result[:n * MAIN].astype(BF16).reshape(n, MAIN, CHUNK)
        extra = result[n * MAIN:].astype(BF16)
        folded = sum(dot(folds[j], extra[:, j * LANES:(j + 1) * LANES]) for j in range(PIECES))
        back_e[k] = folded.reshape(n, FOLD, LANES).astype(BF16)
        for peer in peers:
            for copy in back_copies(k, peer):
                copy.start()
        home_m[k, me] = back_m[k, me]
        home_e[k, me] = back_e[k, me]
        return 0

    lax.fori_loop(0, chunks, finish, 0)

    def collect(k, _):
        for peer in peers:
            for copy in returns(k, peer):
                copy.wait_recv()
        main = dot(put_main, home_m[k].reshape(n * MAIN, CHUNK))
        extras = home_e[k].astype(F32).reshape(n * FOLD, LANES).astype(BF16)
        tail = jnp.concatenate([dot(p, extras) for p in put_extra], axis=1)
        out[k] = (main + tail).astype(BF16)
        out_copy(k).start()
        return 0

    lax.fori_loop(0, chunks, collect, 0)

    def drain(k, _):
        for peer in peers:
            for copy in send_copies(k, peer) + back_copies(k, peer):
                copy.wait_send()
        out_copy(k).wait()
        return 0

    lax.fori_loop(0, chunks, drain, 0)


def local(tokens, expert_ids, combine, w_gate, w_up, w_down):
    n = lax.axis_size("expert")
    span = n // EXPERTS
    count, model_width = tokens.shape
    width = w_gate.shape[1]
    chunks = model_width // CHUNK
    extra_rows = -(-EXTRA * n // MAIN) * MAIN
    rows = n * MAIN + extra_rows
    dma = pltpu.SemaphoreType.DMA
    anywhere = pl.BlockSpec(memory_space=pl.ANY)
    return pl.pallas_call(
        functools.partial(kernel, n, span, chunks),
        out_shape=jax.ShapeDtypeStruct((count, model_width), BF16),
        in_specs=[anywhere] * 6,
        out_specs=anywhere,
        scratch_shapes=[
            pltpu.VMEM((count, model_width), BF16),
            pltpu.VMEM((1, count), I32),
            pltpu.VMEM((1, count), BF16),
            pltpu.VMEM((chunks, CHUNK, width), BF16),
            pltpu.VMEM((chunks, CHUNK, width), BF16),
            pltpu.VMEM((chunks, width, CHUNK), BF16),
            pltpu.VMEM((chunks, n, MAIN, CHUNK), BF16),
            pltpu.VMEM((chunks, n, FOLD, LANES), BF16),
            pltpu.VMEM((chunks, n, MAIN, CHUNK), BF16),
            pltpu.VMEM((chunks, n, FOLD, LANES), BF16),
            pltpu.VMEM((rows, width), F32),
            pltpu.VMEM((rows, width), F32),
            pltpu.VMEM((rows, width), BF16),
            pltpu.VMEM((chunks, count, CHUNK), BF16),
            pltpu.VMEM((chunks, n, MAIN, CHUNK), BF16),
            pltpu.VMEM((chunks, n, FOLD, LANES), BF16),
            pltpu.VMEM((chunks, n, MAIN, CHUNK), BF16),
            pltpu.VMEM((chunks, n, FOLD, LANES), BF16),
            dma((3,)),
            dma((chunks,)),
            dma((chunks,)),
            dma((chunks,)),
            dma((chunks,)),
            dma((chunks, n, 2)),
            dma((chunks, n, 2)),
            dma((chunks, n, 2)),
            dma((chunks, n, 2)),
        ],
        compiler_params=pltpu.CompilerParams(
            collective_id=0, has_side_effects=True, vmem_limit_bytes=60 * 1024 * 1024
        ),
    )(
        tokens,
        expert_ids.reshape(1, count),
        combine.reshape(1, count),
        w_gate,
        w_up,
        w_down,
    )


def solution(mesh):
    placed = (
        P(("dp", "expert"), None),
        P(("dp", "expert"), None),
        P(("dp", "expert"), None),
        P(None, "expert"),
        P(None, "expert"),
        P("expert", None),
    )
    return jax.shard_map(
        local, mesh=mesh, in_specs=placed, out_specs=P(("dp", "expert"), None), check_vma=False
    )
```

```python
import functools

import jax
import jax.numpy as jnp
from jax import lax
from jax.experimental import pallas as pl
from jax.experimental.pallas import tpu as pltpu
from jax.sharding import PartitionSpec as P

EXPERTS = 4
TOP = 1
CAP = 18
MAIN = 16
EXTRA = CAP - MAIN
FOLD = 8
LANES = 128
PIECES = FOLD // EXTRA
CHUNK = PIECES * LANES
BF16, F32, I32 = jnp.bfloat16, jnp.float32, jnp.int32


def iota(shape, axis):
    return lax.broadcasted_iota(I32, shape, axis)


def dot(a, b):
    return jnp.dot(a, b, preferred_element_type=F32)


def kernel(
    n, span, chunks, tokens_hbm, ids_hbm, combine_hbm, gate_hbm, up_hbm, down_hbm, out,
    tokens, ids, combine, gate, up, down, send_m, send_e, recv_m, recv_e, tails, gate_sum, up_sum,
    hidden, back_m, back_e, home_m, home_e,
    small_sem, gate_sem, up_sem, down_sem, send_sem, recv_sem, back_sem, home_sem,
):
    me = lax.axis_index("expert")
    count = tokens.shape[0]
    width = gate.shape[2]
    extra_rows = -(-EXTRA * n // MAIN) * MAIN
    chip, core = me // 2, me % 2

    peers = []
    for step in range(1, n // 2):
        for turn in range(2):
            peers.append((chip + step) % (n // 2) * 2 + (core + turn) % 2)
    peers.append(chip * 2 + (core + 1) % 2)

    barrier = pltpu.get_barrier_semaphore()
    for peer in peers:
        pl.semaphore_signal(barrier, inc=1, device_id={"expert": peer})

    first = [
        pltpu.make_async_copy(ids_hbm, ids, small_sem.at[0]),
        pltpu.make_async_copy(tokens_hbm, tokens, small_sem.at[1]),
        pltpu.make_async_copy(combine_hbm, combine, small_sem.at[2]),
    ]
    for copy in first:
        copy.start()

    def gate_copy(k):
        rows = pl.ds(pl.multiple_of(k * CHUNK, CHUNK), CHUNK)
        return pltpu.make_async_copy(gate_hbm.at[rows, :], gate.at[k], gate_sem.at[k])

    def up_copy(k):
        rows = pl.ds(pl.multiple_of(k * CHUNK, CHUNK), CHUNK)
        return pltpu.make_async_copy(up_hbm.at[rows, :], up.at[k], up_sem.at[k])

    def down_copy(k):
        columns = pl.ds(pl.multiple_of(k * CHUNK, CHUNK), CHUNK)
        return pltpu.make_async_copy(down_hbm.at[:, columns], down.at[k], down_sem.at[k])

    def start_in(k, _):
        gate_copy(k).start()
        up_copy(k).start()
        return 0

    def start_down(k, _):
        down_copy(k).start()
        return 0

    lax.fori_loop(0, chunks, start_in, 0)
    lax.fori_loop(0, chunks, start_down, 0)

    first[0].wait()
    own = ids[...]
    member = iota((8, count), 0) == own
    earlier = (iota((count, count), 0) < iota((count, count), 1)).astype(F32).astype(BF16)
    ranks = dot(member.astype(F32).astype(BF16), earlier)
    place = jnp.sum(jnp.where(member, ranks, 0.0), axis=0, keepdims=True).astype(I32)
    low, high = own * span, own * span + span

    def main_mask():
        row = iota((n * MAIN, count), 0)
        block = row // MAIN
        return (block >= low) & (block < high) & (row - block * MAIN == place)

    def extra_mask(piece):
        row = iota((n * FOLD, count), 0)
        block = row // FOLD
        inner = row - block * FOLD - piece * EXTRA
        return (block >= low) & (block < high) & (inner >= 0) & (inner < EXTRA) & (inner + MAIN == place)

    pick_main = jnp.where(main_mask(), 1.0, 0.0).astype(BF16)
    pick_extra = [jnp.where(extra_mask(j), 1.0, 0.0).astype(BF16) for j in range(PIECES)]

    def send_copies(k, peer, which):
        sources, targets = (send_m, recv_m) if which == 0 else (send_e, recv_e)
        return pltpu.make_async_remote_copy(
            src_ref=sources.at[k, peer], dst_ref=targets.at[k, me],
            send_sem=send_sem.at[k, peer, which], recv_sem=recv_sem.at[k, me, which],
            device_id={"expert": peer},
        )

    def arrivals(k, peer, which):
        sources, targets = (send_m, recv_m) if which == 0 else (send_e, recv_e)
        return pltpu.make_async_remote_copy(
            src_ref=sources.at[k, peer], dst_ref=targets.at[k, peer],
            send_sem=send_sem.at[k, peer, which], recv_sem=recv_sem.at[k, peer, which],
            device_id={"expert": peer},
        )

    def back_copies(k, peer, which):
        sources, targets = (back_m, home_m) if which == 0 else (back_e, home_e)
        return pltpu.make_async_remote_copy(
            src_ref=sources.at[k, peer], dst_ref=targets.at[k, me],
            send_sem=back_sem.at[k, peer, which], recv_sem=home_sem.at[k, me, which],
            device_id={"expert": peer},
        )

    def returns(k, peer, which):
        sources, targets = (back_m, home_m) if which == 0 else (back_e, home_e)
        return pltpu.make_async_remote_copy(
            src_ref=sources.at[k, peer], dst_ref=targets.at[k, peer],
            send_sem=back_sem.at[k, peer, which], recv_sem=home_sem.at[k, peer, which],
            device_id={"expert": peer},
        )

    first[1].wait()
    pl.semaphore_wait(barrier, n - 1)

    def columns_of(k):
        return tokens[:, pl.ds(pl.multiple_of(k * CHUNK, CHUNK), CHUNK)]

    def send_extra(k):
        block = columns_of(k)
        folded = sum(
            dot(pick_extra[j], block[:, j * LANES:(j + 1) * LANES]) for j in range(PIECES)
        )
        send_e[k] = folded.reshape(n, FOLD, LANES).astype(BF16)
        for peer in peers:
            send_copies(k, peer, 1).start()
        recv_e[k, me] = send_e[k, me]

    def send_main(k):
        send_m[k] = dot(pick_main, columns_of(k)).astype(BF16).reshape(n, MAIN, CHUNK)
        for peer in peers:
            send_copies(k, peer, 0).start()
        recv_m[k, me] = send_m[k, me]

    def dispatch(k, _):
        send_extra(k + 1)
        send_main(k)
        return 0

    send_extra(0)
    lax.fori_loop(0, chunks - 1, dispatch, 0)
    send_main(chunks - 1)

    first[2].wait()
    weight = combine[...].astype(F32)
    put_main = jnp.transpose(jnp.where(main_mask(), weight, 0.0)).astype(BF16)
    put_extra = [
        jnp.transpose(jnp.where(extra_mask(j), weight, 0.0)).astype(BF16) for j in range(PIECES)
    ]

    def spread(j):
        row, column = iota((extra_rows, n * FOLD), 0), iota((extra_rows, n * FOLD), 1)
        source = row // EXTRA
        wanted = source * FOLD + j * EXTRA + (row - source * EXTRA)
        return jnp.where(column == wanted, 1.0, 0.0).astype(BF16)

    def fold(j):
        row, column = iota((n * FOLD, extra_rows), 0), iota((n * FOLD, extra_rows), 1)
        source = column // EXTRA
        wanted = source * FOLD + j * EXTRA + (column - source * EXTRA)
        return jnp.where(row == wanted, 1.0, 0.0).astype(BF16)

    spreads = [spread(j) for j in range(PIECES)]
    folds = [fold(j) for j in range(PIECES)]

    def unfold(k):
        extras = recv_e[k].astype(F32).reshape(n * FOLD, LANES).astype(BF16)
        tails[k] = jnp.concatenate([dot(s, extras) for s in spreads], axis=1).astype(BF16)

    def gathered(k):
        return jnp.concatenate([recv_m[k].reshape(n * MAIN, CHUNK), tails[k]], axis=0)

    for peer in peers:
        arrivals(0, peer, 1).wait_recv()
    unfold(0)
    gate_sum[...] = jnp.zeros_like(gate_sum)
    up_sum[...] = jnp.zeros_like(up_sum)

    def project(k, _):
        gate_copy(k).wait()
        up_copy(k).wait()
        for peer in peers:
            arrivals(k + 1, peer, 1).wait_recv()
        for peer in peers:
            arrivals(k, peer, 0).wait_recv()
        rows = gathered(k)
        gate_sum[...] += dot(rows, gate[k])
        up_sum[...] += dot(rows, up[k])
        unfold(k + 1)
        return 0

    lax.fori_loop(0, chunks - 1, project, 0)
    last = chunks - 1
    gate_copy(last).wait()
    up_copy(last).wait()
    for peer in peers:
        arrivals(last, peer, 0).wait_recv()
    rows = gathered(last)
    tile = min(512, width)
    for at in range(0, width, tile):
        part = slice(at, at + tile)
        g = gate_sum[:, part] + dot(rows, gate[last, :, part])
        u = up_sum[:, part] + dot(rows, up[last, :, part])
        hidden[:, part] = (g / (1.0 + jnp.exp(-g)) * u).astype(BF16)

    def finish(k, _):
        down_copy(k).wait()
        result = dot(hidden[...], down[k])
        back_m[k] = result[:n * MAIN].astype(BF16).reshape(n, MAIN, CHUNK)
        for peer in peers:
            back_copies(k, peer, 0).start()
        extra = result[n * MAIN:].astype(BF16)
        folded = sum(dot(folds[j], extra[:, j * LANES:(j + 1) * LANES]) for j in range(PIECES))
        back_e[k] = folded.reshape(n, FOLD, LANES).astype(BF16)
        for peer in peers:
            back_copies(k, peer, 1).start()
        home_m[k, me] = back_m[k, me]
        home_e[k, me] = back_e[k, me]
        return 0

    lax.fori_loop(0, chunks, finish, 0)

    def collect(k, _):
        for peer in peers:
            returns(k, peer, 0).wait_recv()
            returns(k, peer, 1).wait_recv()
        main = dot(put_main, home_m[k].reshape(n * MAIN, CHUNK))
        extras = home_e[k].astype(F32).reshape(n * FOLD, LANES).astype(BF16)
        tail = jnp.concatenate([dot(p, extras) for p in put_extra], axis=1)
        out[:, pl.ds(pl.multiple_of(k * CHUNK, CHUNK), CHUNK)] = (main + tail).astype(BF16)
        return 0

    lax.fori_loop(0, chunks, collect, 0)

    def drain(k, _):
        for peer in peers:
            for which in range(2):
                send_copies(k, peer, which).wait_send()
                back_copies(k, peer, which).wait_send()
        return 0

    lax.fori_loop(0, chunks, drain, 0)


def local(tokens, expert_ids, combine, w_gate, w_up, w_down):
    n = lax.axis_size("expert")
    span = n // EXPERTS
    count, model_width = tokens.shape
    width = w_gate.shape[1]
    chunks = model_width // CHUNK
    extra_rows = -(-EXTRA * n // MAIN) * MAIN
    rows = n * MAIN + extra_rows
    dma = pltpu.SemaphoreType.DMA
    anywhere = pl.BlockSpec(memory_space=pltpu.HBM)
    return pl.pallas_call(
        functools.partial(kernel, n, span, chunks),
        out_shape=jax.ShapeDtypeStruct((count, model_width), BF16),
        in_specs=[anywhere] * 6,
        out_specs=pl.BlockSpec(memory_space=pltpu.VMEM),
        scratch_shapes=[
            pltpu.VMEM((count, model_width), BF16),
            pltpu.VMEM((1, count), I32),
            pltpu.VMEM((1, count), BF16),
            pltpu.VMEM((chunks, CHUNK, width), BF16),
            pltpu.VMEM((chunks, CHUNK, width), BF16),
            pltpu.VMEM((chunks, width, CHUNK), BF16),
            pltpu.VMEM((chunks, n, MAIN, CHUNK), BF16),
            pltpu.VMEM((chunks, n, FOLD, LANES), BF16),
            pltpu.VMEM((chunks, n, MAIN, CHUNK), BF16),
            pltpu.VMEM((chunks, n, FOLD, LANES), BF16),
            pltpu.VMEM((chunks, extra_rows, CHUNK), BF16),
            pltpu.VMEM((rows, width), F32),
            pltpu.VMEM((rows, width), F32),
            pltpu.VMEM((rows, width), BF16),
            pltpu.VMEM((chunks, n, MAIN, CHUNK), BF16),
            pltpu.VMEM((chunks, n, FOLD, LANES), BF16),
            pltpu.VMEM((chunks, n, MAIN, CHUNK), BF16),
            pltpu.VMEM((chunks, n, FOLD, LANES), BF16),
            dma((3,)),
            dma((chunks,)),
            dma((chunks,)),
            dma((chunks,)),
            dma((chunks, n, 2)),
            dma((chunks, n, 2)),
            dma((chunks, n, 2)),
            dma((chunks, n, 2)),
        ],
        compiler_params=pltpu.CompilerParams(
            collective_id=0, vmem_limit_bytes=54 * 1024 * 1024
        ),
    )(
        tokens,
        expert_ids.reshape(1, count),
        combine.reshape(1, count),
        w_gate,
        w_up,
        w_down,
    )


def solution(mesh):
    placed = (
        P(("dp", "expert"), None),
        P(("dp", "expert"), None),
        P(("dp", "expert"), None),
        P(None, "expert"),
        P(None, "expert"),
        P("expert", None),
    )
    return jax.shard_map(
        local, mesh=mesh, in_specs=placed, out_specs=P(("dp", "expert"), None), check_vma=False
    )
```

```python
import functools

import jax
import jax.numpy as jnp
from jax import lax
from jax.experimental import pallas as pl
from jax.experimental.pallas import tpu as pltpu
from jax.sharding import PartitionSpec as P

EXPERTS = 4
TOP = 1
CAP = 18
MAIN = 16
EXTRA = CAP - MAIN
FOLD = 8
LANES = 128
PIECES = FOLD // EXTRA
CHUNK = PIECES * LANES
BF16, F32, I32 = jnp.bfloat16, jnp.float32, jnp.int32


def iota(shape, axis):
    return lax.broadcasted_iota(I32, shape, axis)


def dot(a, b):
    return jnp.dot(a, b, preferred_element_type=F32)


def kernel(
    n, span, chunks, tokens, ids, combine, gate_hbm, up_hbm, down_hbm, out,
    gate, up, down, send_m, send_e, recv_m, recv_e, tails, gate_sum, up_sum,
    hidden, back_m, back_e, home_m, home_e,
    gate_sem, up_sem, down_sem, send_sem, recv_sem, back_sem, home_sem,
):
    me = lax.axis_index("expert")
    count = tokens.shape[0]
    width = gate.shape[2]
    extra_rows = -(-EXTRA * n // MAIN) * MAIN
    chip, core = me // 2, me % 2

    peers = []
    for step in range(1, n // 2):
        for turn in range(2):
            peers.append((chip + step) % (n // 2) * 2 + (core + turn) % 2)
    peers.append(chip * 2 + (core + 1) % 2)

    barrier = pltpu.get_barrier_semaphore()
    for peer in peers:
        pl.semaphore_signal(barrier, inc=1, device_id={"expert": peer})

    def gate_copy(k):
        rows = pl.ds(pl.multiple_of(k * CHUNK, CHUNK), CHUNK)
        return pltpu.make_async_copy(gate_hbm.at[rows, :], gate.at[k], gate_sem.at[k])

    def up_copy(k):
        rows = pl.ds(pl.multiple_of(k * CHUNK, CHUNK), CHUNK)
        return pltpu.make_async_copy(up_hbm.at[rows, :], up.at[k], up_sem.at[k])

    def down_copy(k):
        columns = pl.ds(pl.multiple_of(k * CHUNK, CHUNK), CHUNK)
        return pltpu.make_async_copy(down_hbm.at[:, columns], down.at[k], down_sem.at[k])

    def start_in(k, _):
        gate_copy(k).start()
        up_copy(k).start()
        return 0

    def start_down(k, _):
        down_copy(k).start()
        return 0

    lax.fori_loop(0, chunks, start_in, 0)
    lax.fori_loop(0, chunks, start_down, 0)

    own = ids[...]
    member = iota((8, count), 0) == own
    earlier = (iota((count, count), 0) < iota((count, count), 1)).astype(F32).astype(BF16)
    ranks = dot(member.astype(F32).astype(BF16), earlier)
    place = jnp.sum(jnp.where(member, ranks, 0.0), axis=0, keepdims=True).astype(I32)
    low, high = own * span, own * span + span

    def main_mask():
        row = iota((n * MAIN, count), 0)
        block = row // MAIN
        return (block >= low) & (block < high) & (row - block * MAIN == place)

    def extra_mask(piece):
        row = iota((n * FOLD, count), 0)
        block = row // FOLD
        inner = row - block * FOLD - piece * EXTRA
        return (block >= low) & (block < high) & (inner >= 0) & (inner < EXTRA) & (inner + MAIN == place)

    pick_main = jnp.where(main_mask(), 1.0, 0.0).astype(BF16)
    pick_extra = [jnp.where(extra_mask(j), 1.0, 0.0).astype(BF16) for j in range(PIECES)]

    def send_copies(k, peer, which):
        sources, targets = (send_m, recv_m) if which == 0 else (send_e, recv_e)
        return pltpu.make_async_remote_copy(
            src_ref=sources.at[k, peer], dst_ref=targets.at[k, me],
            send_sem=send_sem.at[k, peer, which], recv_sem=recv_sem.at[k, me, which],
            device_id={"expert": peer},
        )

    def arrivals(k, peer, which):
        sources, targets = (send_m, recv_m) if which == 0 else (send_e, recv_e)
        return pltpu.make_async_remote_copy(
            src_ref=sources.at[k, peer], dst_ref=targets.at[k, peer],
            send_sem=send_sem.at[k, peer, which], recv_sem=recv_sem.at[k, peer, which],
            device_id={"expert": peer},
        )

    def back_copies(k, peer, which):
        sources, targets = (back_m, home_m) if which == 0 else (back_e, home_e)
        return pltpu.make_async_remote_copy(
            src_ref=sources.at[k, peer], dst_ref=targets.at[k, me],
            send_sem=back_sem.at[k, peer, which], recv_sem=home_sem.at[k, me, which],
            device_id={"expert": peer},
        )

    def returns(k, peer, which):
        sources, targets = (back_m, home_m) if which == 0 else (back_e, home_e)
        return pltpu.make_async_remote_copy(
            src_ref=sources.at[k, peer], dst_ref=targets.at[k, peer],
            send_sem=back_sem.at[k, peer, which], recv_sem=home_sem.at[k, peer, which],
            device_id={"expert": peer},
        )

    pl.semaphore_wait(barrier, n - 1)

    def columns_of(k):
        return tokens[:, pl.ds(pl.multiple_of(k * CHUNK, CHUNK), CHUNK)]

    def send_extra(k):
        block = columns_of(k)
        folded = sum(
            dot(pick_extra[j], block[:, j * LANES:(j + 1) * LANES]) for j in range(PIECES)
        )
        send_e[k] = folded.reshape(n, FOLD, LANES).astype(BF16)
        for peer in peers:
            send_copies(k, peer, 1).start()
        recv_e[k, me] = send_e[k, me]

    def send_main(k):
        send_m[k] = dot(pick_main, columns_of(k)).astype(BF16).reshape(n, MAIN, CHUNK)
        for peer in peers:
            send_copies(k, peer, 0).start()
        recv_m[k, me] = send_m[k, me]

    def dispatch(k, _):
        send_extra(k + 1)
        send_main(k)
        return 0

    send_extra(0)
    lax.fori_loop(0, chunks - 1, dispatch, 0)
    send_main(chunks - 1)

    weight = combine[...].astype(F32)
    put_main = jnp.transpose(jnp.where(main_mask(), weight, 0.0)).astype(BF16)
    put_extra = [
        jnp.transpose(jnp.where(extra_mask(j), weight, 0.0)).astype(BF16) for j in range(PIECES)
    ]

    def spread(j):
        row, column = iota((extra_rows, n * FOLD), 0), iota((extra_rows, n * FOLD), 1)
        source = row // EXTRA
        wanted = source * FOLD + j * EXTRA + (row - source * EXTRA)
        return jnp.where(column == wanted, 1.0, 0.0).astype(BF16)

    def fold(j):
        row, column = iota((n * FOLD, extra_rows), 0), iota((n * FOLD, extra_rows), 1)
        source = column // EXTRA
        wanted = source * FOLD + j * EXTRA + (column - source * EXTRA)
        return jnp.where(row == wanted, 1.0, 0.0).astype(BF16)

    spreads = [spread(j) for j in range(PIECES)]
    folds = [fold(j) for j in range(PIECES)]

    def unfold(k):
        extras = recv_e[k].astype(F32).reshape(n * FOLD, LANES).astype(BF16)
        tails[k] = jnp.concatenate([dot(s, extras) for s in spreads], axis=1).astype(BF16)

    def gathered(k):
        return jnp.concatenate([recv_m[k].reshape(n * MAIN, CHUNK), tails[k]], axis=0)

    for peer in peers:
        arrivals(0, peer, 1).wait_recv()
    unfold(0)
    gate_sum[...] = jnp.zeros_like(gate_sum)
    up_sum[...] = jnp.zeros_like(up_sum)

    def project(k, _):
        gate_copy(k).wait()
        up_copy(k).wait()
        for peer in peers:
            arrivals(k + 1, peer, 1).wait_recv()
        for peer in peers:
            arrivals(k, peer, 0).wait_recv()
        rows = gathered(k)
        gate_sum[...] += dot(rows, gate[k])
        up_sum[...] += dot(rows, up[k])
        unfold(k + 1)
        return 0

    lax.fori_loop(0, chunks - 1, project, 0)
    last = chunks - 1
    gate_copy(last).wait()
    up_copy(last).wait()
    for peer in peers:
        arrivals(last, peer, 0).wait_recv()
    rows = gathered(last)
    tile = min(512, width)
    for at in range(0, width, tile):
        part = slice(at, at + tile)
        g = gate_sum[:, part] + dot(rows, gate[last, :, part])
        u = up_sum[:, part] + dot(rows, up[last, :, part])
        hidden[:, part] = (g / (1.0 + jnp.exp(-g)) * u).astype(BF16)

    def finish(k, _):
        down_copy(k).wait()
        result = dot(hidden[...], down[k])
        back_m[k] = result[:n * MAIN].astype(BF16).reshape(n, MAIN, CHUNK)
        for peer in peers:
            back_copies(k, peer, 0).start()
        extra = result[n * MAIN:].astype(BF16)
        folded = sum(dot(folds[j], extra[:, j * LANES:(j + 1) * LANES]) for j in range(PIECES))
        back_e[k] = folded.reshape(n, FOLD, LANES).astype(BF16)
        for peer in peers:
            back_copies(k, peer, 1).start()
        home_m[k, me] = back_m[k, me]
        home_e[k, me] = back_e[k, me]
        return 0

    lax.fori_loop(0, chunks, finish, 0)

    def collect(k, _):
        for peer in peers:
            returns(k, peer, 0).wait_recv()
            returns(k, peer, 1).wait_recv()
        main = dot(put_main, home_m[k].reshape(n * MAIN, CHUNK))
        extras = home_e[k].astype(F32).reshape(n * FOLD, LANES).astype(BF16)
        tail = jnp.concatenate([dot(p, extras) for p in put_extra], axis=1)
        out[:, pl.ds(pl.multiple_of(k * CHUNK, CHUNK), CHUNK)] = (main + tail).astype(BF16)
        return 0

    lax.fori_loop(0, chunks, collect, 0)

    def drain(k, _):
        for peer in peers:
            for which in range(2):
                send_copies(k, peer, which).wait_send()
                back_copies(k, peer, which).wait_send()
        return 0

    lax.fori_loop(0, chunks, drain, 0)


def local(tokens, expert_ids, combine, w_gate, w_up, w_down):
    n = lax.axis_size("expert")
    span = n // EXPERTS
    count, model_width = tokens.shape
    width = w_gate.shape[1]
    chunks = model_width // CHUNK
    extra_rows = -(-EXTRA * n // MAIN) * MAIN
    rows = n * MAIN + extra_rows
    dma = pltpu.SemaphoreType.DMA
    anywhere = pl.BlockSpec(memory_space=pl.ANY)
    return pl.pallas_call(
        functools.partial(kernel, n, span, chunks),
        out_shape=jax.ShapeDtypeStruct((count, model_width), BF16),
        in_specs=[pl.BlockSpec(memory_space=pltpu.VMEM)] * 3 + [anywhere] * 3,
        out_specs=pl.BlockSpec(memory_space=pltpu.VMEM),
        scratch_shapes=[
            pltpu.VMEM((chunks, CHUNK, width), BF16),
            pltpu.VMEM((chunks, CHUNK, width), BF16),
            pltpu.VMEM((chunks, width, CHUNK), BF16),
            pltpu.VMEM((chunks, n, MAIN, CHUNK), BF16),
            pltpu.VMEM((chunks, n, FOLD, LANES), BF16),
            pltpu.VMEM((chunks, n, MAIN, CHUNK), BF16),
            pltpu.VMEM((chunks, n, FOLD, LANES), BF16),
            pltpu.VMEM((chunks, extra_rows, CHUNK), BF16),
            pltpu.VMEM((rows, width), F32),
            pltpu.VMEM((rows, width), F32),
            pltpu.VMEM((rows, width), BF16),
            pltpu.VMEM((chunks, n, MAIN, CHUNK), BF16),
            pltpu.VMEM((chunks, n, FOLD, LANES), BF16),
            pltpu.VMEM((chunks, n, MAIN, CHUNK), BF16),
            pltpu.VMEM((chunks, n, FOLD, LANES), BF16),
            dma((chunks,)),
            dma((chunks,)),
            dma((chunks,)),
            dma((chunks, n, 2)),
            dma((chunks, n, 2)),
            dma((chunks, n, 2)),
            dma((chunks, n, 2)),
        ],
        compiler_params=pltpu.CompilerParams(
            collective_id=0, vmem_limit_bytes=54 * 1024 * 1024
        ),
    )(
        tokens,
        expert_ids.reshape(1, count),
        combine.reshape(1, count),
        w_gate,
        w_up,
        w_down,
    )


def solution(mesh):
    placed = (
        P(("dp", "expert"), None),
        P(("dp", "expert"), None),
        P(("dp", "expert"), None),
        P(None, "expert"),
        P(None, "expert"),
        P("expert", None),
    )
    return jax.shard_map(
        local, mesh=mesh, in_specs=placed, out_specs=P(("dp", "expert"), None), check_vma=False
    )
```

```python
import functools

import jax
import jax.numpy as jnp
from jax import lax
from jax.experimental import pallas as pl
from jax.experimental.pallas import tpu as pltpu
from jax.sharding import PartitionSpec as P

EXPERTS = 4
TOP = 1
CAP = 18
MAIN = 16
EXTRA = CAP - MAIN
FOLD = 8
LANES = 128
PIECES = FOLD // EXTRA
CHUNK = PIECES * LANES
BF16, F32, I32 = jnp.bfloat16, jnp.float32, jnp.int32


def iota(shape, axis):
    return lax.broadcasted_iota(I32, shape, axis)


def dot(a, b):
    return jnp.dot(a, b, preferred_element_type=F32)


def kernel(
    n, span, chunks, tokens_hbm, ids_hbm, combine_hbm, gate_hbm, up_hbm, down_hbm, out,
    tokens, ids, combine, gate, up, down, send_m, send_e, recv_m, recv_e, tails, gate_sum, up_sum,
    hidden, back_m, back_e, home_m, home_e,
    small_sem, gate_sem, up_sem, down_sem, send_sem, recv_sem, back_sem, home_sem,
):
    me = lax.axis_index("expert")
    count = tokens.shape[0]
    width = gate.shape[2]
    extra_rows = -(-EXTRA * n // MAIN) * MAIN
    chip, core = me // 2, me % 2

    peers = []
    for step in range(1, n // 2):
        for turn in range(2):
            peers.append((chip + step) % (n // 2) * 2 + (core + turn) % 2)
    peers.append(chip * 2 + (core + 1) % 2)

    barrier = pltpu.get_barrier_semaphore()
    for peer in peers:
        pl.semaphore_signal(barrier, inc=1, device_id={"expert": peer})

    first = [
        pltpu.make_async_copy(ids_hbm, ids, small_sem.at[0]),
        pltpu.make_async_copy(tokens_hbm, tokens, small_sem.at[1]),
        pltpu.make_async_copy(combine_hbm, combine, small_sem.at[2]),
    ]
    for copy in first:
        copy.start()

    def gate_copy(k):
        rows = pl.ds(pl.multiple_of(k * CHUNK, CHUNK), CHUNK)
        return pltpu.make_async_copy(gate_hbm.at[rows, :], gate.at[k], gate_sem.at[k])

    def up_copy(k):
        rows = pl.ds(pl.multiple_of(k * CHUNK, CHUNK), CHUNK)
        return pltpu.make_async_copy(up_hbm.at[rows, :], up.at[k], up_sem.at[k])

    def down_copy(k):
        columns = pl.ds(pl.multiple_of(k * CHUNK, CHUNK), CHUNK)
        return pltpu.make_async_copy(down_hbm.at[:, columns], down.at[k], down_sem.at[k])

    def start_in(k, _):
        gate_copy(k).start()
        up_copy(k).start()
        return 0

    lax.fori_loop(0, chunks, start_in, 0)

    first[0].wait()
    own = ids[...]
    member = iota((8, count), 0) == own
    earlier = (iota((count, count), 0) < iota((count, count), 1)).astype(F32).astype(BF16)
    ranks = dot(member.astype(F32).astype(BF16), earlier)
    place = jnp.sum(jnp.where(member, ranks, 0.0), axis=0, keepdims=True).astype(I32)
    low, high = own * span, own * span + span

    def main_mask():
        row = iota((n * MAIN, count), 0)
        block = row // MAIN
        return (block >= low) & (block < high) & (row - block * MAIN == place)

    def extra_mask(piece):
        row = iota((n * FOLD, count), 0)
        block = row // FOLD
        inner = row - block * FOLD - piece * EXTRA
        return (block >= low) & (block < high) & (inner >= 0) & (inner < EXTRA) & (inner + MAIN == place)

    pick_main = jnp.where(main_mask(), 1.0, 0.0).astype(BF16)
    pick_extra = [jnp.where(extra_mask(j), 1.0, 0.0).astype(BF16) for j in range(PIECES)]

    def send_copies(k, peer, which):
        sources, targets = (send_m, recv_m) if which == 0 else (send_e, recv_e)
        return pltpu.make_async_remote_copy(
            src_ref=sources.at[k, peer], dst_ref=targets.at[k, me],
            send_sem=send_sem.at[k, peer, which], recv_sem=recv_sem.at[k, me, which],
            device_id={"expert": peer},
        )

    def arrivals(k, peer, which):
        sources, targets = (send_m, recv_m) if which == 0 else (send_e, recv_e)
        return pltpu.make_async_remote_copy(
            src_ref=sources.at[k, peer], dst_ref=targets.at[k, peer],
            send_sem=send_sem.at[k, peer, which], recv_sem=recv_sem.at[k, peer, which],
            device_id={"expert": peer},
        )

    def back_copies(k, peer, which):
        sources, targets = (back_m, home_m) if which == 0 else (back_e, home_e)
        return pltpu.make_async_remote_copy(
            src_ref=sources.at[k, peer], dst_ref=targets.at[k, me],
            send_sem=back_sem.at[k, peer, which], recv_sem=home_sem.at[k, me, which],
            device_id={"expert": peer},
        )

    def returns(k, peer, which):
        sources, targets = (back_m, home_m) if which == 0 else (back_e, home_e)
        return pltpu.make_async_remote_copy(
            src_ref=sources.at[k, peer], dst_ref=targets.at[k, peer],
            send_sem=back_sem.at[k, peer, which], recv_sem=home_sem.at[k, peer, which],
            device_id={"expert": peer},
        )

    first[1].wait()
    pl.semaphore_wait(barrier, n - 1)

    def columns_of(k):
        return tokens[:, pl.ds(pl.multiple_of(k * CHUNK, CHUNK), CHUNK)]

    def send_extra(k):
        block = columns_of(k)
        folded = sum(
            dot(pick_extra[j], block[:, j * LANES:(j + 1) * LANES]) for j in range(PIECES)
        )
        send_e[k] = folded.reshape(n, FOLD, LANES).astype(BF16)
        for peer in peers:
            send_copies(k, peer, 1).start()
        recv_e[k, me] = send_e[k, me]

    def send_main(k):
        send_m[k] = dot(pick_main, columns_of(k)).astype(BF16).reshape(n, MAIN, CHUNK)
        for peer in peers:
            send_copies(k, peer, 0).start()
        recv_m[k, me] = send_m[k, me]

    def dispatch(k, _):
        send_extra(k + 1)
        send_main(k)
        return 0

    send_extra(0)
    lax.fori_loop(0, chunks - 1, dispatch, 0)
    send_main(chunks - 1)

    first[2].wait()
    weight = combine[...].astype(F32)
    put_main = jnp.transpose(jnp.where(main_mask(), weight, 0.0)).astype(BF16)
    put_extra = [
        jnp.transpose(jnp.where(extra_mask(j), weight, 0.0)).astype(BF16) for j in range(PIECES)
    ]

    def spread(j):
        row, column = iota((extra_rows, n * FOLD), 0), iota((extra_rows, n * FOLD), 1)
        source = row // EXTRA
        wanted = source * FOLD + j * EXTRA + (row - source * EXTRA)
        return jnp.where(column == wanted, 1.0, 0.0).astype(BF16)

    def fold(j):
        row, column = iota((n * FOLD, extra_rows), 0), iota((n * FOLD, extra_rows), 1)
        source = column // EXTRA
        wanted = source * FOLD + j * EXTRA + (column - source * EXTRA)
        return jnp.where(row == wanted, 1.0, 0.0).astype(BF16)

    spreads = [spread(j) for j in range(PIECES)]
    folds = [fold(j) for j in range(PIECES)]

    def unfold(k):
        extras = recv_e[k].astype(F32).reshape(n * FOLD, LANES).astype(BF16)
        tails[k] = jnp.concatenate([dot(s, extras) for s in spreads], axis=1).astype(BF16)

    def gathered(k):
        return jnp.concatenate([recv_m[k].reshape(n * MAIN, CHUNK), tails[k]], axis=0)

    for peer in peers:
        arrivals(0, peer, 1).wait_recv()
    unfold(0)
    gate_sum[...] = jnp.zeros_like(gate_sum)
    up_sum[...] = jnp.zeros_like(up_sum)

    def project(k, _):
        gate_copy(k).wait()
        up_copy(k).wait()
        down_copy(k).start()
        for peer in peers:
            arrivals(k + 1, peer, 1).wait_recv()
        for peer in peers:
            arrivals(k, peer, 0).wait_recv()
        rows = gathered(k)
        gate_sum[...] += dot(rows, gate[k])
        up_sum[...] += dot(rows, up[k])
        unfold(k + 1)
        return 0

    lax.fori_loop(0, chunks - 1, project, 0)
    last = chunks - 1
    gate_copy(last).wait()
    up_copy(last).wait()
    down_copy(last).start()
    for peer in peers:
        arrivals(last, peer, 0).wait_recv()
    rows = gathered(last)
    tile = min(512, width)
    for at in range(0, width, tile):
        part = slice(at, at + tile)
        g = gate_sum[:, part] + dot(rows, gate[last, :, part])
        u = up_sum[:, part] + dot(rows, up[last, :, part])
        hidden[:, part] = (g / (1.0 + jnp.exp(-g)) * u).astype(BF16)

    def finish(k, _):
        down_copy(k).wait()
        result = dot(hidden[...], down[k])
        back_m[k] = result[:n * MAIN].astype(BF16).reshape(n, MAIN, CHUNK)
        for peer in peers:
            back_copies(k, peer, 0).start()
        extra = result[n * MAIN:].astype(BF16)
        folded = sum(dot(folds[j], extra[:, j * LANES:(j + 1) * LANES]) for j in range(PIECES))
        back_e[k] = folded.reshape(n, FOLD, LANES).astype(BF16)
        for peer in peers:
            back_copies(k, peer, 1).start()
        home_m[k, me] = back_m[k, me]
        home_e[k, me] = back_e[k, me]
        return 0

    lax.fori_loop(0, chunks, finish, 0)

    def collect(k, _):
        for peer in peers:
            returns(k, peer, 0).wait_recv()
            returns(k, peer, 1).wait_recv()
        main = dot(put_main, home_m[k].reshape(n * MAIN, CHUNK))
        extras = home_e[k].astype(F32).reshape(n * FOLD, LANES).astype(BF16)
        tail = jnp.concatenate([dot(p, extras) for p in put_extra], axis=1)
        out[:, pl.ds(pl.multiple_of(k * CHUNK, CHUNK), CHUNK)] = (main + tail).astype(BF16)
        return 0

    lax.fori_loop(0, chunks, collect, 0)

    def drain(k, _):
        for peer in peers:
            for which in range(2):
                send_copies(k, peer, which).wait_send()
                back_copies(k, peer, which).wait_send()
        return 0

    lax.fori_loop(0, chunks, drain, 0)


def local(tokens, expert_ids, combine, w_gate, w_up, w_down):
    n = lax.axis_size("expert")
    span = n // EXPERTS
    count, model_width = tokens.shape
    width = w_gate.shape[1]
    chunks = model_width // CHUNK
    extra_rows = -(-EXTRA * n // MAIN) * MAIN
    rows = n * MAIN + extra_rows
    dma = pltpu.SemaphoreType.DMA
    anywhere = pl.BlockSpec(memory_space=pltpu.HBM)
    return pl.pallas_call(
        functools.partial(kernel, n, span, chunks),
        out_shape=jax.ShapeDtypeStruct((count, model_width), BF16),
        in_specs=[anywhere] * 6,
        out_specs=pl.BlockSpec(memory_space=pltpu.VMEM),
        scratch_shapes=[
            pltpu.VMEM((count, model_width), BF16),
            pltpu.VMEM((1, count), I32),
            pltpu.VMEM((1, count), BF16),
            pltpu.VMEM((chunks, CHUNK, width), BF16),
            pltpu.VMEM((chunks, CHUNK, width), BF16),
            pltpu.VMEM((chunks, width, CHUNK), BF16),
            pltpu.VMEM((chunks, n, MAIN, CHUNK), BF16),
            pltpu.VMEM((chunks, n, FOLD, LANES), BF16),
            pltpu.VMEM((chunks, n, MAIN, CHUNK), BF16),
            pltpu.VMEM((chunks, n, FOLD, LANES), BF16),
            pltpu.VMEM((chunks, extra_rows, CHUNK), BF16),
            pltpu.VMEM((rows, width), F32),
            pltpu.VMEM((rows, width), F32),
            pltpu.VMEM((rows, width), BF16),
            pltpu.VMEM((chunks, n, MAIN, CHUNK), BF16),
            pltpu.VMEM((chunks, n, FOLD, LANES), BF16),
            pltpu.VMEM((chunks, n, MAIN, CHUNK), BF16),
            pltpu.VMEM((chunks, n, FOLD, LANES), BF16),
            dma((3,)),
            dma((chunks,)),
            dma((chunks,)),
            dma((chunks,)),
            dma((chunks, n, 2)),
            dma((chunks, n, 2)),
            dma((chunks, n, 2)),
            dma((chunks, n, 2)),
        ],
        compiler_params=pltpu.CompilerParams(
            collective_id=0, vmem_limit_bytes=54 * 1024 * 1024
        ),
    )(
        tokens,
        expert_ids.reshape(1, count),
        combine.reshape(1, count),
        w_gate,
        w_up,
        w_down,
    )


def solution(mesh):
    placed = (
        P(("dp", "expert"), None),
        P(("dp", "expert"), None),
        P(("dp", "expert"), None),
        P(None, "expert"),
        P(None, "expert"),
        P("expert", None),
    )
    return jax.shard_map(
        local, mesh=mesh, in_specs=placed, out_specs=P(("dp", "expert"), None), check_vma=False
    )
```
